256 devices in a mesh: seq: 128 (over z, x, y_lo, core), sec: 2 (over y_hi).
Axes of the slice: x: 4, y: 4 (y_hi: 2, y_lo: 2; y = y_hi * 2 + y_lo), z: 8, core: 2. Of those that a mesh axis runs over, the one named last changes fastest.
Arguments:
- queries: bfloat16 [2, 2048, 64, 3072], P('sec', 'seq'), may hold values from -250 to 250
- encoded: bfloat16 [2, 1024, 32, 512], P('sec', 'seq'), may hold values from -6 to 6
- neighbours: int32 [2, 2048, 2], P('sec', 'seq'), may hold values from 0 to 1023, as said below
- kv_weight: bfloat16 [2, 512, 3072], P(None, None, 'seq'), may hold values from -0.25 to 0.25
Outputs:
- attended: bfloat16 [2, 2048, 64, 3072], P('sec', 'seq')
The draws below stay inside these ranges and needn't reach their ends.
Inputs may be any that keep to these rules, and one draw needn't show every extreme that they name: Block id b lies on index b // 8 of seq. The spans held by one device of seq name at most 1 neighbours on any one index of seq, and in every draw some indices of seq receive exactly 1 from every device.
All inputs are finite; a program needn't handle non-finite values.
Results may differ from the reference program's by a relative error of at most 0.012.
Values may be sent and summed in bfloat16 or wider, within the bound.
No kernel may reach another device: no remote copies, remote signals or barrier semaphores. Data moves between devices by JAX's collectives and lax.ppermute only.
A program may use at most 128 MiB of HBM per device.

```python
import jax
import jax.numpy as jnp
from jax import lax

HEADS = 24
HDIM = 128
ENC = 512
CT = 64
NT = 32
SPANS_DEV = 16
BLK_DEV = 8
HD = 3072
SPANS = 2048
BLOCKS = 1024
N_SEQ = 128


def draw_queries(key, part):
    shape = (2, SPANS, CT, HEADS * HDIM)
    first = jax.random.fold_in(key, 0)
    values = jnp.clip(jax.random.normal(first, shape, jnp.float32), -6.0, 6.0)
    return values.astype(jnp.bfloat16)


def draw_neighbours(key, part):
    readers = SPANS // SPANS_DEV
    owners = BLOCKS // BLK_DEV
    cap = (2 * SPANS_DEV + owners - 1) // owners
    hot_count = max(1, owners // 8)
    slots = owners * cap
    order = jax.random.permutation(jax.random.fold_in(key, 7), owners)
    hot = (order < hot_count).astype(jnp.int32)
    owner_of = jnp.arange(slots) // cap
    hot_slot = hot[owner_of]

    def one_device(device_key):
        score_key, shuffle_key, local_key = jax.random.split(device_key, 3)
        score = jax.random.randint(score_key, (slots,), 0, 1 << 20) + hot_slot * (1 << 21)
        score = score * slots + jnp.arange(slots)
        chosen = lax.top_k(score, 2 * SPANS_DEV)[1]
        chosen = jax.random.permutation(shuffle_key, chosen)
        local = jax.random.randint(local_key, (2 * SPANS_DEV,), 0, BLK_DEV)
        return (chosen // cap * BLK_DEV + local).reshape(SPANS_DEV, 2)
    device_keys = jax.random.split(jax.random.fold_in(key, 11), 2 * readers)
    return jax.vmap(one_device)(device_keys).reshape(2, SPANS, 2).astype(jnp.int32)


def level_of(own_key, shape, pieces, low, largest):
    def one(position, parts):
        heights = jax.random.uniform(jax.random.fold_in(jax.random.fold_in(own_key, 6), position), (parts,), jnp.float32, low / len(pieces), largest / len(pieces))
        return jnp.repeat(jnp.exp(heights), shape[position] // parts).reshape((-1,) + (1,) * (len(shape) - position - 1))

    gain = one(*pieces[0])
    for cut in pieces[1:]:
        gain = gain * one(*cut)
    return gain


def centred(own_key, dims, deviation, reach, shards=(), dtype=jnp.bfloat16):
    level = level_of(own_key, dims, shards, -0.22, 0.18) if shards else 1.0
    values = jax.random.normal(own_key, dims, jnp.float32) * deviation * level
    return jnp.minimum(jnp.maximum(values, -reach), reach).astype(dtype)


def setup_inputs(seed: int = 0) -> dict:
    streams_of = jax.random.split(jax.random.key(seed), 5)
    return {
        "queries": draw_queries(jax.random.fold_in(streams_of[4], 71), 0),
        "encoded": centred(streams_of[1], (2, BLOCKS, NT, ENC), 1.0, 6.0, ((0, 2), (1, 128))),
        "neighbours": draw_neighbours(jax.random.fold_in(streams_of[4], 71), 0),
        "kv_weight": centred(streams_of[3], (2, ENC, HD), ENC ** -0.5, 0.25, ((2, 128),)),
    }


def reference(queries, encoded, neighbours, kv_weight):
    results = []
    for section in range(2):
        source = encoded[1 - section].reshape(N_SEQ, BLK_DEV * NT, ENC)

        def project(rows):
            keys = jnp.dot(rows, kv_weight[0], preferred_element_type=jnp.float32).astype(jnp.bfloat16)
            values = jnp.dot(rows, kv_weight[1], preferred_element_type=jnp.float32).astype(jnp.bfloat16)
            return keys, values

        keys_all, values_all = lax.map(project, source)
        keys_all = keys_all.reshape(BLOCKS, NT, HEADS * HDIM)
        values_all = values_all.reshape(BLOCKS, NT, HEADS * HDIM)
        query_groups = queries[section].reshape(N_SEQ, SPANS_DEV, CT, HEADS, HDIM)
        id_groups = neighbours[section].reshape(N_SEQ, SPANS_DEV, 2)

        def attend(pair):
            query_block, id_block = pair
            keys = keys_all[id_block].reshape(SPANS_DEV, 2 * NT, HEADS, HDIM)
            values = values_all[id_block].reshape(SPANS_DEV, 2 * NT, HEADS, HDIM)
            scores = jnp.einsum("cthd,cuhd->chtu", query_block.astype(jnp.float32), keys.astype(jnp.float32)) * (HDIM ** -0.5)
            probs = jax.nn.softmax(scores, axis=-1).astype(jnp.bfloat16)
            mixed = jnp.einsum("chtu,cuhd->cthd", probs.astype(jnp.float32), values.astype(jnp.float32))
            return mixed.astype(jnp.bfloat16)

        output = lax.map(attend, (query_groups, id_groups))
        results.append(output.reshape(SPANS, CT, HEADS * HDIM))
    return jnp.stack(results)
```

```python
import jax
import jax.numpy as jnp
from jax import lax
from jax.experimental import pallas as pl
from jax.experimental.pallas import tpu as pltpu
from jax.sharding import Mesh, PartitionSpec as P

HDIM = 128
NZ, NX, NY, NC = 8, 4, 2, 2
PLANE = NX * NY * NC
NEAR = (0, 1, NZ - 1)
FAR = tuple(range(2, NZ - 1))
PAIR = 2
STEPS = 4
BATCH = 16
SCALE = HDIM ** -0.5
MASKED = -1e30
CONTRACT = (((1,), (1,)), ((), ()))


def shift(count, step):
    return [(i, (i + step) % count) for i in range(count)]


def hop(below, above):
    moved = lax.ppermute(below, "z", shift(NZ, -1)), lax.ppermute(above, "z", shift(NZ, 1))
    return lax.optimization_barrier(moved)


def attend_kernel(near, index, place, q_ref, *refs):
    parts = NZ // STEPS
    own_refs, other_refs = refs[:parts], refs[parts:2 * parts]
    near_rows, far_rows, out_ref, rows, kv, sems = refs[2 * parts:]
    blocks = near.shape[0]
    tokens = rows.shape[0] // blocks
    features = own_refs[0].shape[1]

    def copy(j, source):
        return pltpu.make_async_copy(
            source.at[index[j]], rows.at[pl.ds(j * tokens, tokens)], sems.at[j]
        )

    @pl.when(pl.program_id(0) == 0)
    def _():
        for j in range(blocks):
            @pl.when(near[j] == 1)
            def _():
                copy(j, near_rows).start()

            @pl.when(near[j] == 0)
            def _():
                copy(j, far_rows).start()
        for j in range(blocks):
            copy(j, far_rows).wait()

    core = place[1]
    for part in range(parts):
        at = pl.ds(part * features, features)
        for kind, weight in ((core, own_refs[part]), (1 - core, other_refs[part])):
            kv[kind, :, at] = lax.dot_general(
                rows[...], weight[0], CONTRACT, preferred_element_type=jnp.float32
            ).astype(jnp.bfloat16)

    span = 2 * tokens
    size = PAIR * span
    row = lax.broadcasted_iota(jnp.int32, (size, size), 0) // span
    col = lax.broadcasted_iota(jnp.int32, (size, size), 1) // span
    same = row == col
    ones = jnp.ones((size, HDIM), jnp.bfloat16)
    tiles = [
        (pl.ds(group * size, size), pl.ds(head * HDIM, HDIM))
        for head in range(q_ref.shape[1] // HDIM)
        for group in range(rows.shape[0] // size)
    ]
    for first in range(0, len(tiles), BATCH):
        batch = tiles[first:first + BATCH]
        scores = [
            lax.dot_general(q_ref[tile], kv[(0,) + tile], CONTRACT, preferred_element_type=jnp.float32)
            for tile in batch
        ]
        weights = []
        for score in scores:
            score = jnp.where(same, score * SCALE, MASKED)
            weights.append(jnp.exp(score - jnp.max(score, axis=1, keepdims=True)).astype(jnp.bfloat16))
        for tile, weight in zip(batch, weights):
            both = jnp.concatenate([kv[(1,) + tile], ones], axis=1)
            mixed = jnp.dot(weight, both, preferred_element_type=jnp.float32)
            out_ref[tile] = (mixed[:, :HDIM] / mixed[:, HDIM:]).astype(jnp.bfloat16)


def attend(near, index, place, queries, own, other, near_rows, far_rows):
    tokens, features = queries.shape
    wide = features // STEPS
    parts = NZ // STEPS
    rows = near.shape[0] * near_rows.shape[1]
    width = near_rows.shape[2]
    weight_specs = [
        pl.BlockSpec(
            (1, features // NZ, width),
            lambda g, near, index, place, part=part: ((g * parts + part - place[0]) % NZ, 0, 0),
        )
        for part in range(parts)
    ]
    block = pl.BlockSpec((tokens, wide), lambda g, near, index, place: (0, g))
    whole = pl.BlockSpec(memory_space=pl.ANY)
    return pl.pallas_call(
        attend_kernel,
        out_shape=jax.ShapeDtypeStruct((tokens, features), jnp.bfloat16),
        grid_spec=pltpu.PrefetchScalarGridSpec(
            num_scalar_prefetch=3,
            grid=(STEPS,),
            in_specs=[block] + weight_specs * 2 + [whole, whole],
            out_specs=block,
            scratch_shapes=[
                pltpu.VMEM((rows, width), jnp.bfloat16),
                pltpu.VMEM((2, rows, wide), jnp.bfloat16),
                pltpu.SemaphoreType.DMA((near.shape[0],)),
            ],
        ),
        compiler_params=pltpu.CompilerParams(
            dimension_semantics=("arbitrary",), vmem_limit_bytes=48 << 20
        ),
        cost_estimate=pl.CostEstimate(
            flops=4 * rows * width * features + 8 * tokens * HDIM * features,
            bytes_accessed=4 * tokens * features + 4 * width * features,
            transcendentals=tokens * 128 * features // HDIM,
        ),
    )(near, index, place, queries, *[own] * parts, *[other] * parts, near_rows, far_rows)


def select(pieces, asked, at):
    wanted = jnp.stack([asked[:, ahead] for ahead in at], axis=1)
    wanted = wanted + jnp.arange(len(at))[None, :] * pieces[0].shape[0]
    return jnp.concatenate(pieces)[wanted.reshape(-1)]


def exchange(parcels):
    return lax.all_to_all(parcels, ("x", "y", "c"), split_axis=0, concat_axis=0, tiled=True)


def body(queries, encoded, neighbours, kv_weight):
    plane = ("x", "y", "c")
    blocks_each = encoded.shape[1]
    width = encoded.shape[3]
    z = lax.axis_index("z")
    core = lax.axis_index("c")

    block_ids = neighbours[0].reshape(-1)
    owner = block_ids // blocks_each
    local = block_ids % blocks_each
    column = owner % PLANE
    ahead = (owner // PLANE - z) % NZ
    placed = (column * NZ + ahead)[:, None] == jnp.arange(PLANE * NZ)[None, :]
    request = jnp.sum(jnp.where(placed, local[:, None], 0), 0).reshape(PLANE, NZ)
    near = (ahead < 2) | (ahead == NZ - 1)
    index = jnp.where(
        near, column * len(NEAR) + jnp.minimum(ahead, 2), column * len(FAR) + ahead - 2
    )

    shard = kv_weight.transpose(0, 2, 1)
    columns = shard.shape[1]
    shards = jnp.broadcast_to(shard, (NX * NY,) + shard.shape).reshape((PLANE,) + shard.shape[1:])
    letter = jnp.pad(request.astype(jnp.bfloat16)[:, None, :], ((0, 0), (0, 7), (0, width - NZ)))
    parcel = jnp.concatenate([shards, letter], axis=1)

    here = lax.ppermute(encoded[0], "sec", shift(2, 1))
    here, parcel = lax.optimization_barrier((here, parcel))
    parcel = exchange(parcel)
    asked = parcel[:, columns, :NZ].astype(jnp.int32)
    piece = parcel[:, :columns].reshape(-1, width)
    below1, above1 = hop(here, here)
    near_rows = select([here, below1, above1], asked, NEAR)
    below1, above1, near_rows = lax.optimization_barrier((below1, above1, near_rows))
    near_rows = exchange(near_rows)
    below2, above2 = hop(below1, above1)
    below3, above3 = hop(below2, above2)
    below4 = lax.ppermute(below3, "z", shift(NZ, -1))
    far_rows = select([below2, below3, below4, above3, above2], asked, FAR)
    far_rows, near_rows, piece = lax.optimization_barrier((far_rows, near_rows, piece))
    far_rows = exchange(far_rows)

    w1, v1 = hop(piece, piece)
    w2, v2 = hop(w1, v1)
    w3, v3 = hop(w2, v2)
    w4 = lax.ppermute(w3, "z", shift(NZ, -1))
    pieces = [piece, w1, w2, w3, w4, v3, v2, v1]
    own = jnp.stack(pieces)
    other = jnp.stack([lax.ppermute(part, "c", shift(2, 1)) for part in pieces])

    place = jnp.stack([z, core])
    flat = queries.reshape(-1, queries.shape[3])
    out = attend(near.astype(jnp.int32), index, place, flat, own, other, near_rows, far_rows)
    return out.reshape(queries.shape)


def solution(mesh):
    fine = Mesh(mesh.devices.reshape(NZ, NX, NY, NC, 2), ("z", "x", "y", "c", "sec"))
    seq = ("z", "x", "y", "c")
    placed = (
        P("sec", seq, None, None),
        P("sec", seq, None, None),
        P("sec", seq, None),
        P(None, None, seq),
    )
    return jax.shard_map(
        body, mesh=fine, in_specs=placed, out_specs=P("sec", seq, None, None), check_vma=False
    )
```
